32 devices in a mesh: dp: 2 (over core), ctx: 4 (over z), tp: 4 (over y, x).
Axes of the slice: x: 2, y: 2, z: 4, core: 2. Of those that a mesh axis runs over, the one named last changes fastest.
Arguments:
- block_input: float32 [512, 2, 1024], P(('ctx', 'tp'), 'dp'), may hold values from -6 to 6
- input_gain: float32 [2, 1024], replicated, may hold values from 0.5 to 1.5
- query_weight: bfloat16 [2, 1024, 2048], P(None, None, 'tp'), may hold values from -0.1875 to 0.1875
- key_weight: bfloat16 [2, 1024, 1024], P(None, None, 'tp'), may hold values from -0.1875 to 0.1875
- value_weight: bfloat16 [2, 1024, 1024], P(None, None, 'tp'), may hold values from -0.1875 to 0.1875
- query_gain: float32 [2, 128], replicated, may hold values from 0.1 to 1.9
- key_gain: float32 [2, 128], replicated, may hold values from 0.1 to 1.9
- out_weight: bfloat16 [2, 2048, 1024], P(None, 'tp'), may hold values from -0.75 to 0.75
- post_gain: float32 [2, 1024], replicated, may hold values from 0.5 to 1.5
- gate_weight: bfloat16 [2, 1024, 3072], P(None, None, 'tp'), may hold values from -0.1875 to 0.1875
- up_weight: bfloat16 [2, 1024, 3072], P(None, None, 'tp'), may hold values from -0.1875 to 0.1875
- down_weight: bfloat16 [2, 3072, 1024], P(None, 'tp'), may hold values from -0.109375 to 0.109375
- grad_output: float32 [512, 2, 1024], P(('ctx', 'tp'), 'dp'), may hold values from -6 to 6
Outputs:
- output: float32 [512, 2, 1024], P(('ctx', 'tp'), 'dp')
- grad_input: float32 [512, 2, 1024], P(('ctx', 'tp'), 'dp')
- input_gain_grad: float32 [2, 1024], replicated
- query_weight_grad: float32 [2, 1024, 2048], P(None, ('dp', 'ctx'), 'tp')
- key_weight_grad: float32 [2, 1024, 1024], P(None, ('dp', 'ctx'), 'tp')
- value_weight_grad: float32 [2, 1024, 1024], P(None, ('dp', 'ctx'), 'tp')
- query_gain_grad: float32 [2, 128], replicated
- key_gain_grad: float32 [2, 128], replicated
- out_weight_grad: float32 [2, 2048, 1024], P(None, 'tp', ('dp', 'ctx'))
- post_gain_grad: float32 [2, 1024], replicated
- gate_weight_grad: float32 [2, 1024, 3072], P(None, ('dp', 'ctx'), 'tp')
- up_weight_grad: float32 [2, 1024, 3072], P(None, ('dp', 'ctx'), 'tp')
- down_weight_grad: float32 [2, 3072, 1024], P(None, 'tp', ('dp', 'ctx'))
The draws below stay inside these ranges and needn't reach their ends.
All inputs are finite; a program needn't handle non-finite values.
Results may differ from the reference program's by a relative error of at most 0.034.
Values may be sent and summed in bfloat16 or wider, within the bound.
A program may use at most 192 MiB of HBM per device.

```python
import jax
import jax.numpy as jnp
from jax import lax

D = 1024
HEADS = 16
KV_HEADS = 8
HEAD_DIM = 128
FF = 3072
LAYERS = 2
SEQS = 2
LEN = 512


def block_levels(own_key, extent, split, low, largest):
    def one(axis_at, shards_of):
        draws = jax.random.uniform(jax.random.fold_in(jax.random.fold_in(own_key, 6), axis_at), (shards_of,), jnp.float32, low / len(split), largest / len(split))
        return jnp.repeat(jnp.exp(draws), extent[axis_at] // shards_of).reshape((-1,) + (1,) * (len(extent) - axis_at - 1))

    level = one(*split[0])
    for cut in split[1:]:
        level = level * one(*cut)
    return level


def centred(key, dims, width, limit, cuts=(), held_as=jnp.bfloat16):
    loudness = block_levels(key, dims, cuts, -0.22, 0.18) if cuts else 1.0
    array = jax.random.normal(key, dims, jnp.float32) * width * loudness
    return jnp.minimum(jnp.maximum(array, -limit), limit).astype(held_as)


def setup_inputs(seed: int = 0) -> dict:
    streams_of = jax.random.split(jax.random.key(seed), 14)
    return {
        "block_input": centred(streams_of[0], (LEN, SEQS, D), 1.0, 6.0, ((0, 16), (1, 2)), jnp.float32),
        "input_gain": jnp.clip(1.0 + 0.1 * jax.random.normal(streams_of[1], (LAYERS, D), jnp.float32), 0.5, 1.5),
        "query_weight": centred(streams_of[2], (LAYERS, D, HEADS * HEAD_DIM), D ** -0.5, 0.1875, ((2, 4),)),
        "key_weight": centred(streams_of[3], (LAYERS, D, KV_HEADS * HEAD_DIM), D ** -0.5, 0.1875, ((2, 4),)),
        "value_weight": centred(streams_of[4], (LAYERS, D, KV_HEADS * HEAD_DIM), D ** -0.5, 0.1875, ((2, 4),)),
        "query_gain": jnp.clip(1.0 + 0.18 * jax.random.normal(streams_of[5], (LAYERS, HEAD_DIM), jnp.float32), 0.1, 1.9),
        "key_gain": jnp.clip(1.0 + 0.18 * jax.random.normal(streams_of[6], (LAYERS, HEAD_DIM), jnp.float32), 0.1, 1.9),
        "out_weight": centred(streams_of[7], (LAYERS, HEADS * HEAD_DIM, D), (HEADS * HEAD_DIM // 32) ** -0.5, 0.75, ((1, 4),)),
        "post_gain": jnp.clip(1.0 + 0.1 * jax.random.normal(streams_of[8], (LAYERS, D), jnp.float32), 0.5, 1.5),
        "gate_weight": centred(streams_of[9], (LAYERS, D, FF), D ** -0.5, 0.1875, ((2, 4),)),
        "up_weight": centred(streams_of[10], (LAYERS, D, FF), D ** -0.5, 0.1875, ((2, 4),)),
        "down_weight": centred(streams_of[11], (LAYERS, FF, D), FF ** -0.5, 0.109375, ((1, 4),)),
        "grad_output": centred(streams_of[12], (LEN, SEQS, D), 1.0, 6.0, ((0, 16), (1, 2)), jnp.float32),
    }


EPS = 1e-06
THETA = 1000000.0

def rounded(field):
    return lax.optimization_barrier(field.astype(jnp.bfloat16)).astype(jnp.float32)

def rms_forward(field, gain):
    inverse = lax.rsqrt(lax.optimization_barrier(jnp.mean(field * field, axis=-1, keepdims=True)) + EPS)
    normed = field * inverse
    return (normed * gain, normed, inverse)

def rms_backward(grad_out, normed, inverse, gain):
    leading = tuple(range(grad_out.ndim - 1))
    grad_gain = lax.optimization_barrier(jnp.sum(grad_out * normed, axis=leading))
    scaled = grad_out * gain
    grad_in = inverse * (scaled - normed * lax.optimization_barrier(jnp.mean(scaled * normed, axis=-1, keepdims=True)))
    return (grad_in, grad_gain)

def rope_tables(positions, head_dim):
    half = head_dim // 2
    frequency = THETA ** (-(2.0 * jnp.arange(half, dtype=jnp.float32)) / head_dim)
    angles = positions[:, None] * frequency[None, :]
    angles = jnp.concatenate([angles, angles], axis=-1)
    return (jnp.cos(angles)[:, None, None, :], jnp.sin(angles)[:, None, None, :])

def rotate(field, cosine, sine):
    half = field.shape[-1] // 2
    turned = jnp.concatenate([-field[..., half:], field[..., :half]], axis=-1)
    return field * cosine + turned * sine

def attend_forward(parts):
    query, keys, values = parts
    block = min(512, LEN)
    query_full = query.astype(jnp.float32)
    key_full = keys.astype(jnp.float32)
    value_full = values.astype(jnp.float32)
    key_rows = jnp.arange(LEN).astype(jnp.int32)
    score_scale = HEAD_DIM ** (-0.5)

    def one_block(index):
        start = (index * block).astype(jnp.int32)
        part = lax.dynamic_slice_in_dim(query_full, start, block, 0)
        scores = jnp.einsum('qkgd,tkd->kgqt', part, key_full) * score_scale
        rows = start + jnp.arange(block).astype(jnp.int32)
        scores = jnp.where(key_rows[None, :] <= rows[:, None], scores, -jnp.inf)
        highest = lax.optimization_barrier(jnp.max(scores, axis=-1))
        weights = jnp.exp(scores - highest[..., None])
        total = lax.optimization_barrier(jnp.sum(weights, axis=-1))
        mixed = jnp.einsum('kgqt,tkd->qkgd', rounded(weights), value_full)
        return (mixed / jnp.moveaxis(total, 2, 0)[..., None], highest + jnp.log(total))
    mixed, log_total = lax.map(one_block, jnp.arange(LEN // block).astype(jnp.int32))
    group_size = HEADS // KV_HEADS
    return (mixed.reshape(LEN, KV_HEADS, group_size, HEAD_DIM), jnp.moveaxis(log_total, 0, 2).reshape(KV_HEADS, group_size, LEN))

def attend_backward(parts):
    query, keys, values, heads, log_total, grad_heads = parts
    block = min(512, LEN)
    query_full = query.astype(jnp.float32)
    key_full = keys.astype(jnp.float32)
    value_full = values.astype(jnp.float32)
    grad_full = grad_heads.astype(jnp.float32)
    delta = lax.optimization_barrier(jnp.sum(grad_full * heads.astype(jnp.float32), axis=-1))
    key_rows = jnp.arange(LEN).astype(jnp.int32)
    score_scale = HEAD_DIM ** (-0.5)

    def one_block(carry, index):
        key_acc, value_acc = carry
        start = (index * block).astype(jnp.int32)
        part = lax.dynamic_slice_in_dim(query_full, start, block, 0)
        part_grad = lax.dynamic_slice_in_dim(grad_full, start, block, 0)
        part_lse = lax.dynamic_slice_in_dim(log_total, start, block, 2)
        part_delta = lax.dynamic_slice_in_dim(delta, start, block, 0)
        scores = jnp.einsum('qkgd,tkd->kgqt', part, key_full) * score_scale
        rows = start + jnp.arange(block).astype(jnp.int32)
        scores = jnp.where(key_rows[None, :] <= rows[:, None], scores, -jnp.inf)
        probs = jnp.exp(scores - part_lse[..., None])
        dprob = jnp.einsum('qkgd,tkd->kgqt', part_grad, value_full)
        dscore = rounded(probs * (dprob - jnp.moveaxis(part_delta, 0, 2)[..., None]))
        grad_query = jnp.einsum('kgqt,tkd->qkgd', dscore, key_full) * score_scale
        key_acc = key_acc + jnp.einsum('kgqt,qkgd->tkd', dscore, part) * score_scale
        value_acc = value_acc + jnp.einsum('kgqt,qkgd->tkd', rounded(probs), part_grad)
        return ((key_acc, value_acc), grad_query)
    zero_keys = jnp.zeros((LEN, KV_HEADS, HEAD_DIM), jnp.float32)
    (grad_keys, grad_values), grad_query = lax.scan(one_block, (zero_keys, zero_keys), jnp.arange(LEN // block).astype(jnp.int32))
    return (grad_query.reshape(LEN, KV_HEADS, HEADS // KV_HEADS, HEAD_DIM), grad_keys, grad_values)

def per_sequence(field):
    return jnp.moveaxis(field, 1, 0)

def reference(block_input, input_gain, query_weight, key_weight, value_weight, query_gain, key_gain, out_weight, post_gain, gate_weight, up_weight, down_weight, grad_output):
    group_size = HEADS // KV_HEADS
    rows_all = LEN * SEQS
    cosine, sine = rope_tables(jnp.arange(LEN).astype(jnp.float32), HEAD_DIM)
    hidden = block_input
    kept_all = []
    for index in range(LAYERS):
        normed_one, plain_one, inverse_one = rms_forward(hidden, input_gain[index])
        first_flat = normed_one.astype(jnp.bfloat16).reshape(rows_all, D)
        query = jnp.dot(first_flat, query_weight[index], preferred_element_type=jnp.float32).reshape(LEN, SEQS, HEADS, HEAD_DIM)
        keys = jnp.dot(first_flat, key_weight[index], preferred_element_type=jnp.float32).reshape(LEN, SEQS, KV_HEADS, HEAD_DIM)
        values = jnp.dot(first_flat, value_weight[index], preferred_element_type=jnp.float32).astype(jnp.bfloat16).reshape(LEN, SEQS, KV_HEADS, HEAD_DIM)
        query_normed, query_plain, query_inverse = rms_forward(query, query_gain[index])
        key_normed, key_plain, key_inverse = rms_forward(keys, key_gain[index])
        query_rot = rotate(query_normed, cosine, sine).astype(jnp.bfloat16).reshape(LEN, SEQS, KV_HEADS, group_size, HEAD_DIM)
        key_rot = rotate(key_normed, cosine, sine).astype(jnp.bfloat16)
        attended, log_total = lax.map(attend_forward, (per_sequence(query_rot), per_sequence(key_rot), per_sequence(values)))
        heads_bf = per_sequence(attended).reshape(LEN, SEQS, HEADS * HEAD_DIM).astype(jnp.bfloat16)
        heads_flat = heads_bf.reshape(rows_all, HEADS * HEAD_DIM)
        mixed = hidden + jnp.dot(heads_flat, out_weight[index], preferred_element_type=jnp.float32).reshape(LEN, SEQS, D)
        normed_two, plain_two, inverse_two = rms_forward(mixed, post_gain[index])
        second_flat = normed_two.astype(jnp.bfloat16).reshape(rows_all, D)
        gate = jnp.dot(second_flat, gate_weight[index], preferred_element_type=jnp.float32)
        upward = jnp.dot(second_flat, up_weight[index], preferred_element_type=jnp.float32)
        swish = (jax.nn.silu(gate) * upward).astype(jnp.bfloat16)
        hidden = mixed + jnp.dot(swish, down_weight[index], preferred_element_type=jnp.float32).reshape(LEN, SEQS, D)
        kept_all.append((plain_one, inverse_one, first_flat, query_plain, query_inverse, key_plain, key_inverse, query_rot, key_rot, values, log_total, heads_bf, plain_two, inverse_two, second_flat, gate, upward, swish))
    output = hidden
    grad_hidden = grad_output
    weight_parts = [None] * LAYERS
    gain_parts = [None] * LAYERS
    for index in reversed(range(LAYERS)):
        plain_one, inverse_one, first_flat, query_plain, query_inverse, key_plain, key_inverse, query_rot, key_rot, values, log_total, heads_bf, plain_two, inverse_two, second_flat, gate, upward, swish = kept_all[index]
        grad_rows = grad_hidden.astype(jnp.bfloat16).reshape(rows_all, D)
        grad_swish = jnp.dot(grad_rows, down_weight[index].T, preferred_element_type=jnp.float32)
        down_grad = jnp.dot(swish.T, grad_rows, preferred_element_type=jnp.float32)
        sigma = jax.nn.sigmoid(gate)
        grad_gate = (grad_swish * upward * (sigma * (1.0 + gate * (1.0 - sigma)))).astype(jnp.bfloat16)
        grad_up = (grad_swish * (gate * sigma)).astype(jnp.bfloat16)
        gate_grad = jnp.dot(second_flat.T, grad_gate, preferred_element_type=jnp.float32)
        up_grad = jnp.dot(second_flat.T, grad_up, preferred_element_type=jnp.float32)
        grad_second = jnp.dot(grad_gate, gate_weight[index].T, preferred_element_type=jnp.float32) + jnp.dot(grad_up, up_weight[index].T, preferred_element_type=jnp.float32)
        grad_norm_two, post_part = rms_backward(grad_second.reshape(LEN, SEQS, D), plain_two, inverse_two, post_gain[index])
        grad_mixed = grad_hidden + grad_norm_two
        mixed_rows = grad_mixed.astype(jnp.bfloat16).reshape(rows_all, D)
        grad_heads = jnp.dot(mixed_rows, out_weight[index].T, preferred_element_type=jnp.float32).astype(jnp.bfloat16)
        out_grad = jnp.dot(heads_bf.reshape(rows_all, HEADS * HEAD_DIM).T, mixed_rows, preferred_element_type=jnp.float32)
        grad_grouped = grad_heads.reshape(LEN, SEQS, KV_HEADS, group_size, HEAD_DIM)
        heads_grouped = heads_bf.reshape(LEN, SEQS, KV_HEADS, group_size, HEAD_DIM)
        grad_query, grad_keys, grad_values = lax.map(attend_backward, (per_sequence(query_rot), per_sequence(key_rot), per_sequence(values), per_sequence(heads_grouped), log_total, per_sequence(grad_grouped)))
        grad_query = rotate(per_sequence(grad_query).reshape(LEN, SEQS, HEADS, HEAD_DIM), cosine, -sine)
        grad_keys = rotate(per_sequence(grad_keys), cosine, -sine)
        grad_query, query_part = rms_backward(grad_query, query_plain, query_inverse, query_gain[index])
        grad_keys, key_part = rms_backward(grad_keys, key_plain, key_inverse, key_gain[index])
        query_bf = grad_query.astype(jnp.bfloat16).reshape(rows_all, HEADS * HEAD_DIM)
        key_bf = grad_keys.astype(jnp.bfloat16).reshape(rows_all, KV_HEADS * HEAD_DIM)
        value_bf = per_sequence(grad_values).astype(jnp.bfloat16).reshape(rows_all, KV_HEADS * HEAD_DIM)
        query_grad = jnp.dot(first_flat.T, query_bf, preferred_element_type=jnp.float32)
        key_grad = jnp.dot(first_flat.T, key_bf, preferred_element_type=jnp.float32)
        value_grad = jnp.dot(first_flat.T, value_bf, preferred_element_type=jnp.float32)
        grad_first = jnp.dot(query_bf, query_weight[index].T, preferred_element_type=jnp.float32) + jnp.dot(key_bf, key_weight[index].T, preferred_element_type=jnp.float32) + jnp.dot(value_bf, value_weight[index].T, preferred_element_type=jnp.float32)
        grad_norm_one, input_part = rms_backward(grad_first.reshape(LEN, SEQS, D), plain_one, inverse_one, input_gain[index])
        grad_hidden = grad_mixed + grad_norm_one
        weight_parts[index] = (query_grad, key_grad, value_grad, out_grad, gate_grad, up_grad, down_grad)
        gain_parts[index] = (input_part, query_part, key_part, post_part)
    weights_out = [jnp.stack([part[member] for part in weight_parts]) for member in range(7)]
    gains_out = [jnp.stack([part[member] for part in gain_parts]) for member in range(4)]
    return (output, grad_hidden, gains_out[0], weights_out[0], weights_out[1], weights_out[2], gains_out[1], gains_out[2], weights_out[3], gains_out[3], weights_out[4], weights_out[5], weights_out[6])
```

```python
import functools

import jax
import jax.numpy as jnp
from jax import lax
from jax.experimental import pallas as pl
from jax.experimental.pallas import tpu as pltpu
from jax.sharding import PartitionSpec as P

EPS = 1e-06
THETA = 1000000.0
MESH = pl.DeviceIdType.MESH
F32 = jnp.float32
BF16 = jnp.bfloat16


def rms_forward(field, gain):
    inverse = lax.rsqrt(jnp.mean(field * field, axis=-1, keepdims=True) + EPS)
    normed = field * inverse
    return (normed * gain, normed, inverse)


def rms_backward(grad_out, normed, inverse, gain):
    scaled = grad_out * gain
    return inverse * (scaled - normed * jnp.mean(scaled * normed, axis=-1, keepdims=True))


def rope_tables(positions, head_dim):
    half = head_dim // 2
    frequency = THETA ** (-(2.0 * jnp.arange(half, dtype=F32)) / head_dim)
    angles = positions[:, None] * frequency[None, :]
    angles = jnp.concatenate([angles, angles], axis=-1)
    return (jnp.cos(angles)[:, None, :], jnp.sin(angles)[:, None, :])


def rotate(field, cosine, sine):
    half = field.shape[-1] // 2
    turned = jnp.concatenate([-field[..., half:], field[..., :half]], axis=-1)
    return field * cosine + turned * sine


def remote(src, dst, send, recv, **where):
    return pltpu.make_async_remote_copy(
        src_ref=src,
        dst_ref=dst,
        send_sem=send,
        recv_sem=recv,
        device_id=where,
        device_id_type=MESH,
    )


def boundary_kernel(mode, n_ctx, n_tp, *refs):
    refs = list(refs)
    has_sum = mode != "first"
    has_gather = mode in ("first", "fwd", "bwd")
    partial = refs.pop(0) if has_sum else None
    stream = refs.pop(0)
    gain = refs.pop(0) if mode not in ("fwd_last",) else None
    grad_res = refs.pop(0) if mode in ("bwd", "bwd_last") else None
    fresh = refs.pop(0) if mode != "first" else None
    gain_part = refs.pop(0) if mode in ("bwd", "bwd_last") else None
    out = refs.pop(0) if has_gather else None
    if has_sum:
        landed, rs_send, rs_recv = refs.pop(0), refs.pop(0), refs.pop(0)
    if has_gather:
        own, z_send, z_recv, t_send, t_recv = refs

    me_c = lax.axis_index("ctx")
    me_t = lax.axis_index("tp")
    tp_peers = [lax.rem(me_t + d, n_tp) for d in range(1, n_tp)]
    ctx_peers = [lax.rem(me_c + d, n_ctx) for d in range(1, n_ctx)] if has_gather else []
    barrier = pltpu.get_barrier_semaphore()
    for peer in tp_peers:
        pl.semaphore_signal(barrier, inc=1, device_id={"tp": peer}, device_id_type=MESH)
    for peer in ctx_peers:
        pl.semaphore_signal(barrier, inc=1, device_id={"ctx": peer}, device_id_type=MESH)
    pl.semaphore_wait(barrier, len(tp_peers) + len(ctx_peers))

    if has_sum:
        sums = [
            remote(partial.at[peer], landed.at[d], rs_send.at[d], rs_recv.at[d], tp=peer)
            for d, peer in enumerate(tp_peers)
        ]
        for copy in sums:
            copy.start()
        total = partial[me_t].astype(F32)
        for d, copy in enumerate(sums):
            copy.wait_recv()
            total = total + landed[d].astype(F32)
        for copy in sums:
            copy.wait_send()

    field = stream[...]
    if mode == "first":
        sent = rms_forward(field, gain[...])[0].astype(BF16)
    elif mode in ("fwd", "fwd_last"):
        field = field + total
        fresh[...] = field
        if mode == "fwd":
            sent = rms_forward(field, gain[...])[0].astype(BF16)
    else:
        _, normed, inverse = rms_forward(field, gain[...])
        gain_part[...] = jnp.sum(total * normed, axis=0, keepdims=True)
        field = grad_res[...] + rms_backward(total, normed, inverse, gain[...])
        fresh[...] = field
        sent = field.astype(BF16)

    if has_gather:
        own[...] = sent
        copies = []
        for d, peer in enumerate(ctx_peers):
            copies.append(
                remote(own, out.at[me_c, me_t], z_send.at[d], z_recv.at[d], ctx=peer)
            )
        for d, peer in enumerate(tp_peers):
            copies.append(
                remote(own, out.at[me_c, me_t], t_send.at[0, d], t_recv.at[0, d], tp=peer)
            )
        for copy in copies:
            copy.start()
        out[me_c, me_t] = sent
        for d in range(n_ctx - 1):
            source = lax.rem(me_c + n_ctx - (d + 1), n_ctx)
            slot = out.at[source, me_t]
            remote(own, slot, z_send.at[d], z_recv.at[d], ctx=source).wait_recv()
            for k, peer in enumerate(tp_peers):
                copy = remote(slot, slot, t_send.at[d + 1, k], t_recv.at[d + 1, k], tp=peer)
                copy.start()
                copies.append(copy)
        for d in range(n_ctx):
            source = lax.rem(me_c + n_ctx - d, n_ctx)
            for k in range(n_tp - 1):
                origin = lax.rem(me_t + n_tp - (k + 1), n_tp)
                remote(
                    own, out.at[source, origin], t_send.at[d, k], t_recv.at[d, k], tp=origin
                ).wait_recv()
        for copy in copies:
            copy.wait_send()


IDS = {"first": 0, "fwd": 1, "fwd_last": 2, "bwd": 3, "bwd_last": 4}


def boundary(mode, stream, gain=None, partial=None, grad_res=None):
    n_ctx, n_tp = lax.axis_size("ctx"), lax.axis_size("tp")
    rows, width = stream.shape
    operands = []
    if partial is not None:
        operands.append(partial.reshape(n_tp, rows, width))
    operands.append(stream)
    if gain is not None:
        operands.append(gain.reshape(1, width))
    if grad_res is not None:
        operands.append(grad_res)
    shapes = []
    if mode != "first":
        shapes.append(jax.ShapeDtypeStruct((rows, width), F32))
    if grad_res is not None:
        shapes.append(jax.ShapeDtypeStruct((1, width), F32))
    scratch = []
    dma = pltpu.SemaphoreType.DMA
    if partial is not None:
        scratch += [pltpu.VMEM((n_tp - 1, rows, width), BF16), dma((n_tp - 1,)), dma((n_tp - 1,))]
    if mode in ("first", "fwd", "bwd"):
        shapes.append(jax.ShapeDtypeStruct((n_ctx, n_tp, rows, width), BF16))
        scratch += [
            pltpu.VMEM((rows, width), BF16),
            dma((n_ctx - 1,)),
            dma((n_ctx - 1,)),
            dma((n_ctx, n_tp - 1)),
            dma((n_ctx, n_tp - 1)),
        ]
    vmem = pl.BlockSpec(memory_space=pltpu.VMEM)
    outs = pl.pallas_call(
        functools.partial(boundary_kernel, mode, n_ctx, n_tp),
        out_shape=shapes,
        in_specs=[vmem] * len(operands),
        out_specs=[vmem] * len(shapes),
        scratch_shapes=scratch,
        name="boundary_" + mode,
        compiler_params=pltpu.CompilerParams(
            collective_id=IDS[mode], has_side_effects=True, vmem_limit_bytes=32 * 2**20
        ),
    )(*operands)
    outs = list(outs)
    if mode in ("first", "fwd", "bwd"):
        outs[-1] = outs[-1].reshape(n_ctx * n_tp * rows, width)
    return outs


def gains_kernel(sizes, x_ref, o_ref, cur, land_0, land_1, land_2, send, recv):
    lands = (land_0, land_1, land_2)
    axes = list(sizes)
    barrier = pltpu.get_barrier_semaphore()
    peers = {}
    count = 0
    for axis in axes:
        me = lax.axis_index(axis)
        peers[axis] = [lax.rem(me + d, sizes[axis]) for d in range(1, sizes[axis])]
        for peer in peers[axis]:
            pl.semaphore_signal(barrier, inc=1, device_id={axis: peer}, device_id_type=MESH)
            count += 1
    pl.semaphore_wait(barrier, count)
    total = x_ref[...]
    base = 0
    for step, axis in enumerate(axes):
        cur[step] = total
        copies = [
            remote(
                cur.at[step], lands[step].at[d], send.at[base + d], recv.at[base + d], **{axis: peer}
            )
            for d, peer in enumerate(peers[axis])
        ]
        for copy in copies:
            copy.start()
        me = lax.axis_index(axis)
        parts = []
        for d, copy in enumerate(copies):
            copy.wait_recv()
        acc = jnp.zeros_like(total)
        for position in range(sizes[axis]):
            offset = lax.rem(me + sizes[axis] - position, sizes[axis])
            slot = jnp.maximum(offset - 1, 0)
            acc = acc + jnp.where(offset == 0, total, lands[step][slot])
        total = acc
        for copy in copies:
            copy.wait_send()
        base += len(copies)
    o_ref[...] = total


def sum_gains(x):
    sizes = {axis: lax.axis_size(axis) for axis in ("dp", "ctx", "tp")}
    count = sum(n - 1 for n in sizes.values())
    vmem = pl.BlockSpec(memory_space=pltpu.VMEM)
    return pl.pallas_call(
        functools.partial(gains_kernel, sizes),
        out_shape=jax.ShapeDtypeStruct(x.shape, F32),
        in_specs=[vmem],
        out_specs=vmem,
        scratch_shapes=[pltpu.VMEM((3,) + x.shape, F32)]
        + [pltpu.VMEM((max(n - 1, 1),) + x.shape, F32) for n in sizes.values()]
        + [pltpu.SemaphoreType.DMA((count,)), pltpu.SemaphoreType.DMA((count,))],
        name="sum_gains",
        compiler_params=pltpu.CompilerParams(collective_id=5, has_side_effects=True),
    )(x)


NT = (((1,), (1,)), ((), ()))
NN = (((1,), (0,)), ((), ()))
TN = (((0,), (0,)), ((), ()))


def dot(a, b, dims):
    return lax.dot_general(a, b, dims, preferred_element_type=F32)


def soft_weights(scale, bq, q, k):
    rows = pl.program_id(2) * bq + lax.broadcasted_iota(jnp.int32, (bq, k.shape[0]), 0)
    cols = lax.broadcasted_iota(jnp.int32, (bq, k.shape[0]), 1)
    scores = jnp.where(cols <= rows, dot(q, k, NT) * scale, -jnp.inf)
    weights = jnp.exp(scores - jnp.max(scores, axis=-1, keepdims=True))
    return weights, jnp.sum(weights, axis=-1, keepdims=True)


def attend_kernel(scale, bq, q_ref, k_ref, v_ref, o_ref):
    weights, total = soft_weights(scale, bq, q_ref[...], k_ref[...])
    o_ref[...] = (dot(weights.astype(BF16), v_ref[...], NN) / total).astype(BF16)


def attend_back_kernel(scale, bq, q_ref, k_ref, v_ref, o_ref, do_ref, dq_ref, dk_ref, dv_ref):
    q, k, do = q_ref[...], k_ref[...], do_ref[...]
    weights, total = soft_weights(scale, bq, q, k)
    probs = weights / total
    delta = jnp.sum(do.astype(F32) * o_ref[...].astype(F32), axis=-1, keepdims=True)
    dscore = (probs * (dot(do, v_ref[...], NT) - delta)).astype(BF16)
    dq_ref[...] = dot(dscore, k, NN) * scale

    @pl.when((pl.program_id(1) == 0) & (pl.program_id(2) == 0))
    def _():
        dk_ref[...] = jnp.zeros_like(dk_ref)
        dv_ref[...] = jnp.zeros_like(dv_ref)

    dk_ref[...] += dot(dscore, q, TN) * scale
    dv_ref[...] += dot(probs.astype(BF16), do, TN)


def attention(back, scale, group, head_dim, *operands):
    length, kv_width = operands[1].shape
    kv_heads = kv_width // head_dim
    bq = min(length, 256)
    rows = pl.BlockSpec((bq, head_dim), lambda h, g, i: (i, h * group + g))
    keys = pl.BlockSpec((length, head_dim), lambda h, g, i: (0, h))
    wide = jax.ShapeDtypeStruct((length, kv_width * group), F32 if back else BF16)
    narrow = jax.ShapeDtypeStruct((length, kv_width), F32)
    work = 2 * length * length * head_dim * kv_heads * group
    return pl.pallas_call(
        functools.partial(attend_back_kernel if back else attend_kernel, scale, bq),
        grid=(kv_heads, group, length // bq),
        out_shape=(wide, narrow, narrow) if back else wide,
        in_specs=[rows, keys, keys] + ([rows, rows] if back else []),
        out_specs=(rows, keys, keys) if back else rows,
        name="attend_back" if back else "attend",
        cost_estimate=pl.CostEstimate(
            flops=work * (5 if back else 2), bytes_accessed=4 * length * 1024, transcendentals=0
        ),
        compiler_params=pltpu.CompilerParams(vmem_limit_bytes=32 * 2**20),
    )(*operands)


def on_device(
    block_input,
    input_gain,
    query_weight,
    key_weight,
    value_weight,
    query_gain,
    key_gain,
    out_weight,
    post_gain,
    gate_weight,
    up_weight,
    down_weight,
    grad_output,
):
    local_rows, seq_local, width = block_input.shape
    assert seq_local == 1 and lax.axis_size("dp") == 2
    layers = input_gain.shape[0]
    head_dim = query_gain.shape[-1]
    heads = query_weight.shape[-1] // head_dim
    kv_heads = key_weight.shape[-1] // head_dim
    n_ctx, n_tp = lax.axis_size("ctx"), lax.axis_size("tp")
    block_rows = local_rows * n_tp
    length = block_rows * n_ctx
    scale = head_dim ** (-0.5)
    first_row = lax.axis_index("ctx") * block_rows
    cosine, sine = rope_tables(jnp.arange(length, dtype=F32), head_dim)
    piece = width // (2 * n_ctx)
    my_cols = (lax.axis_index("dp") * n_ctx + lax.axis_index("ctx")) * piece
    other_cols = ((1 - lax.axis_index("dp")) * n_ctx + lax.axis_index("ctx")) * piece
    swap = [(0, 1), (1, 0)]

    def mine(x):
        return lax.dynamic_slice_in_dim(x, first_row, block_rows, 0)

    def slices(x):
        parts = [lax.dynamic_slice_in_dim(x, at, piece, 1) for at in (my_cols, other_cols)]
        return jnp.concatenate(parts, axis=1)

    def settle(grad, axis):
        own, other = jnp.split(grad, 2, axis=axis)
        return own + lax.ppermute(other.astype(BF16), "dp", swap).astype(F32)

    def heads_of(x, count):
        return x.reshape(length, count, head_dim)

    attend_args = (scale, heads // kv_heads, head_dim)
    hidden = block_input[:, 0]
    grad_hidden = grad_output[:, 0]
    grad_rows = lax.all_gather(grad_hidden.astype(BF16), ("ctx", "tp"), axis=0, tiled=True)
    (first_in,) = boundary("first", hidden, input_gain[0])
    kept = []
    for l in range(layers):
        query = dot(first_in, query_weight[l], NN)
        keys = dot(first_in, key_weight[l], NN)
        values = dot(first_in, value_weight[l], NN).astype(BF16)
        query_normed, q_plain, q_inv = rms_forward(heads_of(query, heads), query_gain[l])
        key_normed, k_plain, k_inv = rms_forward(heads_of(keys, kv_heads), key_gain[l])
        query_rot = rotate(query_normed, cosine, sine).astype(BF16).reshape(length, -1)
        key_rot = rotate(key_normed, cosine, sine).astype(BF16).reshape(length, -1)
        attended = attention(False, *attend_args, query_rot, key_rot, values)
        partial = dot(mine(attended), out_weight[l], NN).astype(BF16)
        mixed, second_in = boundary("fwd", hidden, post_gain[l], partial)
        gate = dot(second_in, gate_weight[l], NN)
        upward = dot(second_in, up_weight[l], NN)
        swish = (jax.nn.silu(gate) * upward).astype(BF16)
        partial = dot(mine(swish), down_weight[l], NN).astype(BF16)
        kept.append(
            (hidden, first_in, q_plain, q_inv, k_plain, k_inv, query_rot, key_rot, values)
            + (attended, mixed, second_in, gate, upward, swish)
        )
        if l + 1 < layers:
            hidden, first_in = boundary("fwd", mixed, input_gain[l + 1], partial)
        else:
            (hidden,) = boundary("fwd_last", mixed, None, partial)

    grads = [None] * layers
    gains = [None] * layers
    for l in reversed(range(layers)):
        (x_in, first_in, q_plain, q_inv, k_plain, k_inv, query_rot, key_rot, values) = kept[l][:9]
        attended, mixed, second_in, gate, upward, swish = kept[l][9:]
        grad_swish = dot(grad_rows, down_weight[l], NT)
        sigma = jax.nn.sigmoid(gate)
        grad_gate = (grad_swish * upward * (sigma * (1.0 + gate * (1.0 - sigma)))).astype(BF16)
        grad_up = (grad_swish * (gate * sigma)).astype(BF16)
        partial = dot(mine(grad_gate), gate_weight[l], NT) + dot(mine(grad_up), up_weight[l], NT)
        grad_mixed, post_part, mixed_rows = boundary(
            "bwd", mixed, post_gain[l], partial.astype(BF16), grad_hidden
        )
        second_cols = slices(second_in)
        down_grad = settle(dot(swish, slices(grad_rows), TN), 1)
        gate_grad = settle(dot(second_cols, grad_gate, TN), 0)
        up_grad = settle(dot(second_cols, grad_up, TN), 0)

        grad_heads = dot(mixed_rows, out_weight[l], NT).astype(BF16)
        out_grad = settle(dot(attended, slices(mixed_rows), TN), 1)
        grad_query, grad_keys, grad_values = attention(
            True, *attend_args, query_rot, key_rot, values, attended, grad_heads
        )
        grad_query = rotate(heads_of(grad_query, heads), cosine, -sine)
        grad_keys = rotate(heads_of(grad_keys, kv_heads), cosine, -sine)
        q_part = jnp.sum(mine(grad_query * q_plain), axis=(0, 1))
        k_part = jnp.sum(mine(grad_keys * k_plain), axis=(0, 1))
        query_bf = rms_backward(grad_query, q_plain, q_inv, query_gain[l]).astype(BF16)
        key_bf = rms_backward(grad_keys, k_plain, k_inv, key_gain[l]).astype(BF16)
        query_bf = query_bf.reshape(length, -1)
        key_bf = key_bf.reshape(length, -1)
        value_bf = grad_values.astype(BF16)
        partial = (
            dot(mine(query_bf), query_weight[l], NT)
            + dot(mine(key_bf), key_weight[l], NT)
            + dot(mine(value_bf), value_weight[l], NT)
        ).astype(BF16)
        if l:
            grad_hidden, input_part, grad_rows = boundary(
                "bwd", x_in, input_gain[l], partial, grad_mixed
            )
        else:
            grad_hidden, input_part = boundary(
                "bwd_last", x_in, input_gain[l], partial, grad_mixed
            )
        first_cols = slices(first_in)
        query_grad = settle(dot(first_cols, query_bf, TN), 0)
        key_grad = settle(dot(first_cols, key_bf, TN), 0)
        value_grad = settle(dot(first_cols, value_bf, TN), 0)
        grads[l] = (query_grad, key_grad, value_grad, out_grad, gate_grad, up_grad, down_grad)
        gains[l] = (input_part[0], q_part, k_part, post_part[0])
    stacked = [jnp.stack([part[m] for part in grads]) for m in range(7)]
    packed = jnp.concatenate([v for part in gains for v in part])
    sizes = [v.shape[0] for part in gains for v in part]
    padded = -(-packed.shape[0] // 1024) * 1024
    packed = jnp.pad(packed, (0, padded - packed.shape[0])).reshape(-1, 128)
    summed = sum_gains(packed).reshape(-1)
    pieces = []
    at = 0
    for size in sizes:
        pieces.append(summed[at : at + size])
        at += size
    gains = [jnp.stack([pieces[4 * l + m] for l in range(layers)]) for m in range(4)]
    return (
        hidden[:, None],
        grad_hidden[:, None],
        gains[0],
        stacked[0],
        stacked[1],
        stacked[2],
        gains[1],
        gains[2],
        stacked[3],
        gains[3],
        stacked[4],
        stacked[5],
        stacked[6],
    )


def solution(mesh):
    placed = (
        P(("ctx", "tp"), "dp", None),
        P(),
        P(None, None, "tp"),
        P(None, None, "tp"),
        P(None, None, "tp"),
        P(),
        P(),
        P(None, "tp", None),
        P(),
        P(None, None, "tp"),
        P(None, None, "tp"),
        P(None, "tp", None),
        P(("ctx", "tp"), "dp", None),
    )
    return jax.shard_map(
        on_device,
        mesh=mesh,
        in_specs=placed,
        out_specs=(
            P(("ctx", "tp"), "dp", None),
            P(("ctx", "tp"), "dp", None),
            P(),
            P(None, ("dp", "ctx"), "tp"),
            P(None, ("dp", "ctx"), "tp"),
            P(None, ("dp", "ctx"), "tp"),
            P(),
            P(),
            P(None, "tp", ("dp", "ctx")),
            P(),
            P(None, ("dp", "ctx"), "tp"),
            P(None, ("dp", "ctx"), "tp"),
            P(None, "tp", ("dp", "ctx")),
        ),
        check_vma=False,
    )
```

```python
import functools

import jax
import jax.numpy as jnp
from jax import lax
from jax.experimental import pallas as pl
from jax.experimental.pallas import tpu as pltpu
from jax.sharding import PartitionSpec as P

EPS = 1e-06
THETA = 1000000.0
MESH = pl.DeviceIdType.MESH
F32 = jnp.float32
BF16 = jnp.bfloat16


def rms_forward(field, gain):
    inverse = lax.rsqrt(jnp.mean(field * field, axis=-1, keepdims=True) + EPS)
    normed = field * inverse
    return (normed * gain, normed, inverse)


def rms_backward(grad_out, normed, inverse, gain):
    scaled = grad_out * gain
    return inverse * (scaled - normed * jnp.mean(scaled * normed, axis=-1, keepdims=True))


def rope_tables(positions, head_dim):
    half = head_dim // 2
    frequency = THETA ** (-(2.0 * jnp.arange(half, dtype=F32)) / head_dim)
    angles = positions[:, None] * frequency[None, :]
    cosine, sine = jnp.cos(angles), jnp.sin(angles)
    return (jnp.concatenate([cosine, cosine], axis=-1), jnp.concatenate([-sine, sine], axis=-1))


def remote(src, dst, send, recv, **where):
    return pltpu.make_async_remote_copy(
        src_ref=src,
        dst_ref=dst,
        send_sem=send,
        recv_sem=recv,
        device_id=where,
        device_id_type=MESH,
    )


def boundary_kernel(mode, n_ctx, n_tp, *refs):
    refs = list(refs)
    has_sum = mode != "first"
    has_gather = mode in ("first", "fwd", "bwd")
    partial = refs.pop(0) if has_sum else None
    stream = refs.pop(0)
    gain = refs.pop(0) if mode not in ("fwd_last",) else None
    grad_res = refs.pop(0) if mode in ("bwd", "bwd_last") else None
    fresh = refs.pop(0) if mode != "first" else None
    gain_part = refs.pop(0) if mode in ("bwd", "bwd_last") else None
    out = refs.pop(0) if has_gather else None
    if has_sum:
        landed, rs_send, rs_recv = refs.pop(0), refs.pop(0), refs.pop(0)
    if has_gather:
        own, z_send, z_recv, t_send, t_recv = refs

    me_c = lax.axis_index("ctx")
    me_t = lax.axis_index("tp")
    tp_peers = [lax.rem(me_t + d, n_tp) for d in range(1, n_tp)]
    ctx_peers = [lax.rem(me_c + d, n_ctx) for d in range(1, n_ctx)] if has_gather else []
    barrier = pltpu.get_barrier_semaphore()
    side = me_t + 1 - 2 * lax.rem(me_t, 2)
    over = lax.rem(me_t + 2, n_tp)
    cross = lax.rem(side + 2, n_tp)
    greeted = tp_peers if has_sum else [side, over]
    for peer in greeted:
        pl.semaphore_signal(barrier, inc=1, device_id={"tp": peer}, device_id_type=MESH)
    for peer in ctx_peers:
        pl.semaphore_signal(barrier, inc=1, device_id={"ctx": peer}, device_id_type=MESH)
    pl.semaphore_wait(barrier, len(greeted) + len(ctx_peers))

    if has_sum:
        sums = [
            remote(partial.at[peer], landed.at[d], rs_send.at[d], rs_recv.at[d], tp=peer)
            for d, peer in enumerate(tp_peers)
        ]
        for copy in sums:
            copy.start()
        total = partial[me_t].astype(F32)
        for d, copy in enumerate(sums):
            copy.wait_recv()
            total = total + landed[d].astype(F32)
        for copy in sums:
            copy.wait_send()

    field = stream[...]
    if mode == "first":
        sent = rms_forward(field, gain[...])[0].astype(BF16)
    elif mode in ("fwd", "fwd_last"):
        field = field + total
        fresh[...] = field
        if mode == "fwd":
            sent = rms_forward(field, gain[...])[0].astype(BF16)
    else:
        _, normed, inverse = rms_forward(field, gain[...])
        gain_part[...] = jnp.sum(total * normed, axis=0, keepdims=True)
        field = grad_res[...] + rms_backward(total, normed, inverse, gain[...])
        fresh[...] = field
        sent = field.astype(BF16)

    if has_gather:
        own[...] = sent
        half = own.shape[0] // 2
        order = sorted(range(1, n_ctx), key=lambda d: min(2 * d - 1, 2 * (n_ctx - d)))
        copies = []
        for d in order:
            peer = ctx_peers[d - 1]
            copies.append(
                remote(
                    own, out.at[me_c, me_t], z_send.at[d - 1], z_recv.at[d - 1], ctx=peer
                )
            )
            copies[-1].start()

        def place(d, origin):
            return out.at[lax.rem(me_c + n_ctx - d, n_ctx), origin]

        def send(src, dst, d, k, peer):
            copies.append(remote(src, dst, t_send.at[d, k], t_recv.at[d, k], tp=peer))
            copies[-1].start()

        def arrive(dst, d, k, peer):
            remote(dst, dst, t_send.at[d, k], t_recv.at[d, k], tp=peer).wait_recv()

        def spread(d):
            src = own if d == 0 else place(d, me_t)
            send(src, place(d, me_t), d, 0, side)
            send(src, place(d, me_t), d, 1, over)

        def relay(d):
            arrive(place(d, side), d, 0, side)
            upper = place(d, side).at[pl.ds(0, half)]
            send(upper, upper, d, 2, over)
            arrive(place(d, over), d, 1, over)
            lower = place(d, over).at[pl.ds(half, half)]
            send(lower, lower, d, 3, side)

        spread(0)
        out[me_c, me_t] = sent
        behind = 0
        for d in order:
            source = lax.rem(me_c + n_ctx - d, n_ctx)
            remote(own, place(d, me_t), z_send.at[d - 1], z_recv.at[d - 1], ctx=source).wait_recv()
            spread(d)
            relay(behind)
            behind = d
        relay(behind)
        for d in [0] + order:
            arrive(place(d, cross).at[pl.ds(0, half)], d, 2, over)
            arrive(place(d, cross).at[pl.ds(half, half)], d, 3, side)
        for copy in copies:
            copy.wait_send()


IDS = {"first": 0, "fwd": 1, "fwd_last": 2, "bwd": 3, "bwd_last": 4}


def boundary(mode, stream, gain=None, partial=None, grad_res=None):
    n_ctx, n_tp = lax.axis_size("ctx"), lax.axis_size("tp")
    rows, width = stream.shape
    operands = []
    if partial is not None:
        operands.append(partial.reshape(n_tp, rows, width))
    operands.append(stream)
    if gain is not None:
        operands.append(gain.reshape(1, width))
    if grad_res is not None:
        operands.append(grad_res)
    shapes = []
    if mode != "first":
        shapes.append(jax.ShapeDtypeStruct((rows, width), F32))
    if grad_res is not None:
        shapes.append(jax.ShapeDtypeStruct((1, width), F32))
    scratch = []
    dma = pltpu.SemaphoreType.DMA
    if partial is not None:
        scratch += [pltpu.VMEM((n_tp - 1, rows, width), BF16), dma((n_tp - 1,)), dma((n_tp - 1,))]
    if mode in ("first", "fwd", "bwd"):
        shapes.append(jax.ShapeDtypeStruct((n_ctx, n_tp, rows, width), BF16))
        scratch += [
            pltpu.VMEM((rows, width), BF16),
            dma((n_ctx - 1,)),
            dma((n_ctx - 1,)),
            dma((n_ctx, 4)),
            dma((n_ctx, 4)),
        ]
    vmem = pl.BlockSpec(memory_space=pltpu.VMEM)
    outs = pl.pallas_call(
        functools.partial(boundary_kernel, mode, n_ctx, n_tp),
        out_shape=shapes,
        in_specs=[vmem] * len(operands),
        out_specs=[vmem] * len(shapes),
        scratch_shapes=scratch,
        name="boundary_" + mode,
        compiler_params=pltpu.CompilerParams(
            collective_id=IDS[mode], has_side_effects=True, vmem_limit_bytes=32 * 2**20
        ),
    )(*operands)
    outs = list(outs)
    if mode in ("first", "fwd", "bwd"):
        outs[-1] = outs[-1].reshape(n_ctx * n_tp * rows, width)
    return outs


def gains_kernel(sizes, x_ref, o_ref, cur, land_0, land_1, land_2, send, recv):
    lands = (land_0, land_1, land_2)
    axes = list(sizes)
    barrier = pltpu.get_barrier_semaphore()
    peers = {}
    count = 0
    for axis in axes:
        me = lax.axis_index(axis)
        peers[axis] = [lax.rem(me + d, sizes[axis]) for d in range(1, sizes[axis])]
        for peer in peers[axis]:
            pl.semaphore_signal(barrier, inc=1, device_id={axis: peer}, device_id_type=MESH)
            count += 1
    pl.semaphore_wait(barrier, count)
    total = x_ref[...]
    base = 0
    for step, axis in enumerate(axes):
        cur[step] = total
        copies = [
            remote(
                cur.at[step], lands[step].at[d], send.at[base + d], recv.at[base + d], **{axis: peer}
            )
            for d, peer in enumerate(peers[axis])
        ]
        for copy in copies:
            copy.start()
        me = lax.axis_index(axis)
        parts = []
        for d, copy in enumerate(copies):
            copy.wait_recv()
        acc = jnp.zeros_like(total)
        for position in range(sizes[axis]):
            offset = lax.rem(me + sizes[axis] - position, sizes[axis])
            slot = jnp.maximum(offset - 1, 0)
            acc = acc + jnp.where(offset == 0, total, lands[step][slot])
        total = acc
        for copy in copies:
            copy.wait_send()
        base += len(copies)
    o_ref[...] = total


def sum_gains(x):
    sizes = {axis: lax.axis_size(axis) for axis in ("dp", "ctx", "tp")}
    count = sum(n - 1 for n in sizes.values())
    vmem = pl.BlockSpec(memory_space=pltpu.VMEM)
    return pl.pallas_call(
        functools.partial(gains_kernel, sizes),
        out_shape=jax.ShapeDtypeStruct(x.shape, F32),
        in_specs=[vmem],
        out_specs=vmem,
        scratch_shapes=[pltpu.VMEM((3,) + x.shape, F32)]
        + [pltpu.VMEM((max(n - 1, 1),) + x.shape, F32) for n in sizes.values()]
        + [pltpu.SemaphoreType.DMA((count,)), pltpu.SemaphoreType.DMA((count,))],
        name="sum_gains",
        compiler_params=pltpu.CompilerParams(collective_id=5, has_side_effects=True),
    )(x)


NT = (((1,), (1,)), ((), ()))
NN = (((1,), (0,)), ((), ()))
TN = (((0,), (0,)), ((), ()))


def dot(a, b, dims):
    return lax.dot_general(a, b, dims, preferred_element_type=F32)


def turn(x):
    return pltpu.roll(x, x.shape[-1] // 2, axis=1)


def prepared(x, gain, cosine, sine):
    normed, plain, inverse = rms_forward(x, gain)
    return (normed * cosine + turn(normed) * sine).astype(BF16), plain, inverse


def soft_weights(scale, bq, q, k):
    rows = pl.program_id(2) * bq + lax.broadcasted_iota(jnp.int32, (bq, k.shape[0]), 0)
    cols = lax.broadcasted_iota(jnp.int32, (bq, k.shape[0]), 1)
    scores = jnp.where(cols <= rows, dot(q, k, NT) * scale, -jnp.inf)
    weights = jnp.exp(scores - jnp.max(scores, axis=-1, keepdims=True))
    return weights, jnp.sum(weights, axis=-1, keepdims=True)


def attend_kernel(
    scale, bq, q_ref, k_ref, v_ref, cq_ref, sq_ref, ck_ref, sk_ref, qg_ref, kg_ref, o_ref, k_rot
):
    @pl.when((pl.program_id(1) == 0) & (pl.program_id(2) == 0))
    def _():
        k_rot[...] = prepared(k_ref[...], kg_ref[...], ck_ref[...], sk_ref[...])[0]

    q = prepared(q_ref[...], qg_ref[...], cq_ref[...], sq_ref[...])[0]
    weights, total = soft_weights(scale, bq, q, k_rot[...])
    o_ref[...] = (dot(weights.astype(BF16), v_ref[...], NN) / total).astype(BF16)


def attend_back_kernel(
    scale,
    bq,
    q_ref,
    k_ref,
    v_ref,
    cq_ref,
    sq_ref,
    ck_ref,
    sk_ref,
    qg_ref,
    kg_ref,
    o_ref,
    do_ref,
    dq_ref,
    dk_ref,
    dv_ref,
    qp_ref,
    kp_ref,
    k_rot,
    dk_sum,
    dv_sum,
):
    head, member, block = pl.program_id(0), pl.program_id(1), pl.program_id(2)

    @pl.when((head == 0) & (member == 0) & (block == 0))
    def _():
        qp_ref[...] = jnp.zeros_like(qp_ref)
        kp_ref[...] = jnp.zeros_like(kp_ref)

    @pl.when((member == 0) & (block == 0))
    def _():
        k_rot[...] = prepared(k_ref[...], kg_ref[...], ck_ref[...], sk_ref[...])[0]
        dk_sum[...] = jnp.zeros_like(dk_sum)
        dv_sum[...] = jnp.zeros_like(dv_sum)

    q, plain, inverse = prepared(q_ref[...], qg_ref[...], cq_ref[...], sq_ref[...])
    k, do = k_rot[...], do_ref[...]
    weights, total = soft_weights(scale, bq, q, k)
    probs = weights / total
    delta = jnp.sum(do.astype(F32) * o_ref[...].astype(F32), axis=-1, keepdims=True)
    dscore = (probs * (dot(do, v_ref[...], NT) - delta)).astype(BF16)
    dk_sum[...] += dot(dscore, q, TN) * scale
    dv_sum[...] += dot(probs.astype(BF16), do, TN)
    grad = dot(dscore, k, NN) * scale
    grad = grad * cq_ref[...] - turn(grad) * sq_ref[...]
    qp_ref[...] += jnp.sum(grad * plain, axis=0, keepdims=True)
    dq_ref[...] = rms_backward(grad, plain, inverse, qg_ref[...]).astype(BF16)

    @pl.when((member == pl.num_programs(1) - 1) & (block == pl.num_programs(2) - 1))
    def _():
        _, k_plain, k_inverse = prepared(k_ref[...], kg_ref[...], ck_ref[...], sk_ref[...])
        grad_k = dk_sum[...]
        grad_k = grad_k * ck_ref[...] - turn(grad_k) * sk_ref[...]
        kp_ref[...] += jnp.sum(grad_k * k_plain, axis=0, keepdims=True)
        dk_ref[...] = rms_backward(grad_k, k_plain, k_inverse, kg_ref[...]).astype(BF16)
        dv_ref[...] = dv_sum[...].astype(BF16)


def attention(scale, group, query, keys, values, cosine, sine, query_gain, key_gain, *back):
    length, kv_width = keys.shape
    head_dim = cosine.shape[-1]
    kv_heads = kv_width // head_dim
    bq = min(length, 256)
    rows = pl.BlockSpec((bq, head_dim), lambda h, g, i: (i, h * group + g))
    keyed = pl.BlockSpec((length, head_dim), lambda h, g, i: (0, h))
    table_q = pl.BlockSpec((bq, head_dim), lambda h, g, i: (i, 0))
    table_k = pl.BlockSpec((length, head_dim), lambda h, g, i: (0, 0))
    flat = pl.BlockSpec((1, head_dim), lambda h, g, i: (0, 0))
    wide = jax.ShapeDtypeStruct((length, kv_width * group), BF16)
    narrow = jax.ShapeDtypeStruct((length, kv_width), BF16)
    part = jax.ShapeDtypeStruct((1, head_dim), F32)
    work = 2 * length * length * head_dim * kv_heads * group
    scratch = [pltpu.VMEM((length, head_dim), BF16)]
    if back:
        scratch += [pltpu.VMEM((length, head_dim), F32)] * 2
    return pl.pallas_call(
        functools.partial(attend_back_kernel if back else attend_kernel, scale, bq),
        grid=(kv_heads, group, length // bq),
        out_shape=(wide, narrow, narrow, part, part) if back else wide,
        in_specs=[rows, keyed, keyed, table_q, table_q, table_k, table_k, flat, flat]
        + [rows] * len(back),
        out_specs=(rows, keyed, keyed, flat, flat) if back else rows,
        scratch_shapes=scratch,
        name="attend_back" if back else "attend",
        cost_estimate=pl.CostEstimate(
            flops=work * (5 if back else 2), bytes_accessed=4 * length * 1024, transcendentals=0
        ),
        compiler_params=pltpu.CompilerParams(vmem_limit_bytes=40 * 2**20),
    )(
        query,
        keys,
        values,
        cosine,
        sine,
        cosine,
        sine,
        query_gain.reshape(1, -1),
        key_gain.reshape(1, -1),
        *back,
    )


def on_device(
    block_input,
    input_gain,
    query_weight,
    key_weight,
    value_weight,
    query_gain,
    key_gain,
    out_weight,
    post_gain,
    gate_weight,
    up_weight,
    down_weight,
    grad_output,
):
    local_rows, seq_local, width = block_input.shape
    assert seq_local == 1 and lax.axis_size("dp") == 2 and lax.axis_size("tp") == 4
    layers = input_gain.shape[0]
    head_dim = query_gain.shape[-1]
    heads = query_weight.shape[-1] // head_dim
    kv_heads = key_weight.shape[-1] // head_dim
    n_ctx, n_tp = lax.axis_size("ctx"), lax.axis_size("tp")
    block_rows = local_rows * n_tp
    length = block_rows * n_ctx
    scale = head_dim ** (-0.5)
    first_row = lax.axis_index("ctx") * block_rows
    cosine, sine = rope_tables(jnp.arange(length, dtype=F32), head_dim)
    piece = width // (2 * n_ctx)
    my_cols = (lax.axis_index("dp") * n_ctx + lax.axis_index("ctx")) * piece
    other_cols = ((1 - lax.axis_index("dp")) * n_ctx + lax.axis_index("ctx")) * piece
    swap = [(0, 1), (1, 0)]

    def mine(x):
        return lax.dynamic_slice_in_dim(x, first_row, block_rows, 0)

    def slices(x):
        parts = [lax.dynamic_slice_in_dim(x, at, piece, 1) for at in (my_cols, other_cols)]
        return jnp.concatenate(parts, axis=1)

    def settle(grad, axis):
        own, other = jnp.split(grad, 2, axis=axis)
        return own + lax.ppermute(other.astype(BF16), "dp", swap).astype(F32)

    def settle_rows(*products):
        other = [x[piece:].astype(BF16) for x in products]
        other = lax.ppermute(jnp.concatenate(other, axis=1), "dp", swap).astype(F32)
        out = []
        at = 0
        for x in products:
            out.append(x[:piece] + other[:, at : at + x.shape[1]])
            at += x.shape[1]
        return out

    hidden = block_input[:, 0]
    grad_hidden = grad_output[:, 0]
    grad_rows = lax.all_gather(grad_hidden.astype(BF16), ("ctx", "tp"), axis=0, tiled=True)
    (first_in,) = boundary("first", hidden, input_gain[0])
    kept = []
    for l in range(layers):
        query = dot(first_in, query_weight[l], NN)
        keys = dot(first_in, key_weight[l], NN)
        values = dot(first_in, value_weight[l], NN).astype(BF16)
        attend_args = (scale, heads // kv_heads, query, keys, values, cosine, sine)
        attend_args += (query_gain[l], key_gain[l])
        attended = attention(*attend_args)
        partial = dot(mine(attended), out_weight[l], NN).astype(BF16)
        mixed, second_in = boundary("fwd", hidden, post_gain[l], partial)
        gate = dot(second_in, gate_weight[l], NN)
        upward = dot(second_in, up_weight[l], NN)
        swish = (jax.nn.silu(gate) * upward).astype(BF16)
        partial = dot(mine(swish), down_weight[l], NN).astype(BF16)
        kept.append(
            (hidden, first_in, attend_args, attended, mixed, second_in, gate, upward, swish)
        )
        if l + 1 < layers:
            hidden, first_in = boundary("fwd", mixed, input_gain[l + 1], partial)
        else:
            hidden = mixed + lax.psum_scatter(
                partial, "tp", scatter_dimension=0, tiled=True
            ).astype(F32)

    grads = [None] * layers
    gains = [None] * layers
    for l in reversed(range(layers)):
        x_in, first_in, attend_args, attended, mixed, second_in, gate, upward, swish = kept[l]
        grad_swish = dot(grad_rows, down_weight[l], NT)
        sigma = jax.nn.sigmoid(gate)
        grad_gate = (grad_swish * upward * (sigma * (1.0 + gate * (1.0 - sigma)))).astype(BF16)
        grad_up = (grad_swish * (gate * sigma)).astype(BF16)
        partial = dot(mine(grad_gate), gate_weight[l], NT) + dot(mine(grad_up), up_weight[l], NT)
        grad_mixed, post_part, mixed_rows = boundary(
            "bwd", mixed, post_gain[l], partial.astype(BF16), grad_hidden
        )
        second_cols = slices(second_in)
        down_grad = settle(dot(swish, slices(grad_rows), TN), 1)
        gate_grad, up_grad = settle_rows(
            dot(second_cols, grad_gate, TN), dot(second_cols, grad_up, TN)
        )

        grad_heads = dot(mixed_rows, out_weight[l], NT).astype(BF16)
        out_grad = settle(dot(attended, slices(mixed_rows), TN), 1)
        query_bf, key_bf, value_bf, q_part, k_part = attention(*attend_args, attended, grad_heads)
        partial = (
            dot(mine(query_bf), query_weight[l], NT)
            + dot(mine(key_bf), key_weight[l], NT)
            + dot(mine(value_bf), value_weight[l], NT)
        ).astype(BF16)
        if l:
            grad_hidden, input_part, grad_rows = boundary(
                "bwd", x_in, input_gain[l], partial, grad_mixed
            )
        else:
            grad_hidden, input_part = boundary(
                "bwd_last", x_in, input_gain[l], partial, grad_mixed
            )
        first_cols = slices(first_in)
        query_grad, key_grad, value_grad = settle_rows(
            dot(first_cols, query_bf, TN),
            dot(first_cols, key_bf, TN),
            dot(first_cols, value_bf, TN),
        )
        grads[l] = (query_grad, key_grad, value_grad, out_grad, gate_grad, up_grad, down_grad)
        gains[l] = (input_part[0], q_part[0] / n_ctx, k_part[0] / n_ctx, post_part[0])
    stacked = [jnp.stack([part[m] for part in grads]) for m in range(7)]
    packed = jnp.concatenate([v for part in gains for v in part])
    sizes = [v.shape[0] for part in gains for v in part]
    padded = -(-packed.shape[0] // 1024) * 1024
    packed = jnp.pad(packed, (0, padded - packed.shape[0])).reshape(-1, 128)
    summed = sum_gains(packed).reshape(-1)
    pieces = []
    at = 0
    for size in sizes:
        pieces.append(summed[at : at + size])
        at += size
    gains = [jnp.stack([pieces[4 * l + m] for l in range(layers)]) for m in range(4)]
    return (
        hidden[:, None],
        grad_hidden[:, None],
        gains[0],
        stacked[0],
        stacked[1],
        stacked[2],
        gains[1],
        gains[2],
        stacked[3],
        gains[3],
        stacked[4],
        stacked[5],
        stacked[6],
    )


def solution(mesh):
    placed = (
        P(("ctx", "tp"), "dp", None),
        P(),
        P(None, None, "tp"),
        P(None, None, "tp"),
        P(None, None, "tp"),
        P(),
        P(),
        P(None, "tp", None),
        P(),
        P(None, None, "tp"),
        P(None, None, "tp"),
        P(None, "tp", None),
        P(("ctx", "tp"), "dp", None),
    )
    return jax.shard_map(
        on_device,
        mesh=mesh,
        in_specs=placed,
        out_specs=(
            P(("ctx", "tp"), "dp", None),
            P(("ctx", "tp"), "dp", None),
            P(),
            P(None, ("dp", "ctx"), "tp"),
            P(None, ("dp", "ctx"), "tp"),
            P(None, ("dp", "ctx"), "tp"),
            P(),
            P(),
            P(None, "tp", ("dp", "ctx")),
            P(),
            P(None, ("dp", "ctx"), "tp"),
            P(None, ("dp", "ctx"), "tp"),
            P(None, "tp", ("dp", "ctx")),
        ),
        check_vma=False,
    )
```

```python
import functools

import jax
import jax.numpy as jnp
from jax import lax
from jax.experimental import pallas as pl
from jax.experimental.pallas import tpu as pltpu
from jax.sharding import PartitionSpec as P

EPS = 1e-06
THETA = 1000000.0
MESH = pl.DeviceIdType.MESH
F32 = jnp.float32
BF16 = jnp.bfloat16


def rms_forward(field, gain):
    inverse = lax.rsqrt(jnp.mean(field * field, axis=-1, keepdims=True) + EPS)
    normed = field * inverse
    return (normed * gain, normed, inverse)


def rms_backward(grad_out, normed, inverse, gain):
    scaled = grad_out * gain
    return inverse * (scaled - normed * jnp.mean(scaled * normed, axis=-1, keepdims=True))


def rope_tables(positions, head_dim):
    half = head_dim // 2
    frequency = THETA ** (-(2.0 * jnp.arange(half, dtype=F32)) / head_dim)
    angles = positions[:, None] * frequency[None, :]
    cosine, sine = jnp.cos(angles), jnp.sin(angles)
    return (jnp.concatenate([cosine, cosine], axis=-1), jnp.concatenate([-sine, sine], axis=-1))


def remote(src, dst, send, recv, **where):
    return pltpu.make_async_remote_copy(
        src_ref=src,
        dst_ref=dst,
        send_sem=send,
        recv_sem=recv,
        device_id=where,
        device_id_type=MESH,
    )


def boundary_kernel(mode, n_ctx, n_tp, *refs):
    refs = list(refs)
    has_sum = mode != "first"
    has_gather = mode in ("first", "fwd", "bwd")
    partial = refs.pop(0) if has_sum else None
    stream = refs.pop(0)
    gain = refs.pop(0) if mode not in ("fwd_last",) else None
    grad_res = refs.pop(0) if mode in ("bwd", "bwd_last") else None
    fresh = refs.pop(0) if mode != "first" else None
    gain_part = refs.pop(0) if mode in ("bwd", "bwd_last") else None
    out = refs.pop(0) if has_gather else None
    if has_sum:
        landed, rs_send, rs_recv = refs.pop(0), refs.pop(0), refs.pop(0)
    if has_gather:
        own, z_send, z_recv, t_send, t_recv = refs

    me_c = lax.axis_index("ctx")
    me_t = lax.axis_index("tp")
    tp_peers = [lax.rem(me_t + d, n_tp) for d in range(1, n_tp)]
    ctx_peers = [lax.rem(me_c + d, n_ctx) for d in range(1, n_ctx)] if has_gather else []
    barrier = pltpu.get_barrier_semaphore()
    for peer in tp_peers:
        pl.semaphore_signal(barrier, inc=1, device_id={"tp": peer}, device_id_type=MESH)
    for peer in ctx_peers:
        pl.semaphore_signal(barrier, inc=1, device_id={"ctx": peer}, device_id_type=MESH)
    pl.semaphore_wait(barrier, len(tp_peers) + len(ctx_peers))

    if has_sum:
        sums = [
            remote(partial.at[peer], landed.at[d], rs_send.at[d], rs_recv.at[d], tp=peer)
            for d, peer in enumerate(tp_peers)
        ]
        for copy in sums:
            copy.start()
        total = partial[me_t].astype(F32)
        for d, copy in enumerate(sums):
            copy.wait_recv()
            total = total + landed[d].astype(F32)
        for copy in sums:
            copy.wait_send()

    field = stream[...]
    if mode == "first":
        sent = rms_forward(field, gain[...])[0].astype(BF16)
    elif mode in ("fwd", "fwd_last"):
        field = field + total
        fresh[...] = field
        if mode == "fwd":
            sent = rms_forward(field, gain[...])[0].astype(BF16)
    else:
        _, normed, inverse = rms_forward(field, gain[...])
        gain_part[...] = jnp.sum(total * normed, axis=0, keepdims=True)
        field = grad_res[...] + rms_backward(total, normed, inverse, gain[...])
        fresh[...] = field
        sent = field.astype(BF16)

    if has_gather:
        own[...] = sent
        copies = []
        for d, peer in enumerate(ctx_peers):
            copies.append(
                remote(own, out.at[me_c, me_t], z_send.at[d], z_recv.at[d], ctx=peer)
            )
        for d, peer in enumerate(tp_peers):
            copies.append(
                remote(own, out.at[me_c, me_t], t_send.at[0, d], t_recv.at[0, d], tp=peer)
            )
        for copy in copies:
            copy.start()
        out[me_c, me_t] = sent
        for d in range(n_ctx - 1):
            source = lax.rem(me_c + n_ctx - (d + 1), n_ctx)
            slot = out.at[source, me_t]
            remote(own, slot, z_send.at[d], z_recv.at[d], ctx=source).wait_recv()
            for k, peer in enumerate(tp_peers):
                copy = remote(slot, slot, t_send.at[d + 1, k], t_recv.at[d + 1, k], tp=peer)
                copy.start()
                copies.append(copy)
        for d in range(n_ctx):
            source = lax.rem(me_c + n_ctx - d, n_ctx)
            for k in range(n_tp - 1):
                origin = lax.rem(me_t + n_tp - (k + 1), n_tp)
                remote(
                    own, out.at[source, origin], t_send.at[d, k], t_recv.at[d, k], tp=origin
                ).wait_recv()
        for copy in copies:
            copy.wait_send()


IDS = {"first": 0, "fwd": 1, "fwd_last": 2, "bwd": 3, "bwd_last": 4}


def boundary(mode, stream, gain=None, partial=None, grad_res=None):
    n_ctx, n_tp = lax.axis_size("ctx"), lax.axis_size("tp")
    rows, width = stream.shape
    operands = []
    if partial is not None:
        operands.append(partial.reshape(n_tp, rows, width))
    operands.append(stream)
    if gain is not None:
        operands.append(gain.reshape(1, width))
    if grad_res is not None:
        operands.append(grad_res)
    shapes = []
    if mode != "first":
        shapes.append(jax.ShapeDtypeStruct((rows, width), F32))
    if grad_res is not None:
        shapes.append(jax.ShapeDtypeStruct((1, width), F32))
    scratch = []
    dma = pltpu.SemaphoreType.DMA
    if partial is not None:
        scratch += [pltpu.VMEM((n_tp - 1, rows, width), BF16), dma((n_tp - 1,)), dma((n_tp - 1,))]
    if mode in ("first", "fwd", "bwd"):
        shapes.append(jax.ShapeDtypeStruct((n_ctx, n_tp, rows, width), BF16))
        scratch += [
            pltpu.VMEM((rows, width), BF16),
            dma((n_ctx - 1,)),
            dma((n_ctx - 1,)),
            dma((n_ctx, n_tp - 1)),
            dma((n_ctx, n_tp - 1)),
        ]
    vmem = pl.BlockSpec(memory_space=pltpu.VMEM)
    outs = pl.pallas_call(
        functools.partial(boundary_kernel, mode, n_ctx, n_tp),
        out_shape=shapes,
        in_specs=[vmem] * len(operands),
        out_specs=[vmem] * len(shapes),
        scratch_shapes=scratch,
        name="boundary_" + mode,
        compiler_params=pltpu.CompilerParams(
            collective_id=IDS[mode], has_side_effects=True, vmem_limit_bytes=32 * 2**20
        ),
    )(*operands)
    outs = list(outs)
    if mode in ("first", "fwd", "bwd"):
        outs[-1] = outs[-1].reshape(n_ctx * n_tp * rows, width)
    return outs


def gains_kernel(sizes, x_ref, o_ref, cur, land_0, land_1, land_2, send, recv):
    lands = (land_0, land_1, land_2)
    axes = list(sizes)
    barrier = pltpu.get_barrier_semaphore()
    peers = {}
    count = 0
    for axis in axes:
        me = lax.axis_index(axis)
        peers[axis] = [lax.rem(me + d, sizes[axis]) for d in range(1, sizes[axis])]
        for peer in peers[axis]:
            pl.semaphore_signal(barrier, inc=1, device_id={axis: peer}, device_id_type=MESH)
            count += 1
    pl.semaphore_wait(barrier, count)
    total = x_ref[...]
    base = 0
    for step, axis in enumerate(axes):
        cur[step] = total
        copies = [
            remote(
                cur.at[step], lands[step].at[d], send.at[base + d], recv.at[base + d], **{axis: peer}
            )
            for d, peer in enumerate(peers[axis])
        ]
        for copy in copies:
            copy.start()
        me = lax.axis_index(axis)
        parts = []
        for d, copy in enumerate(copies):
            copy.wait_recv()
        acc = jnp.zeros_like(total)
        for position in range(sizes[axis]):
            offset = lax.rem(me + sizes[axis] - position, sizes[axis])
            slot = jnp.maximum(offset - 1, 0)
            acc = acc + jnp.where(offset == 0, total, lands[step][slot])
        total = acc
        for copy in copies:
            copy.wait_send()
        base += len(copies)
    o_ref[...] = total


def sum_gains(x):
    sizes = {axis: lax.axis_size(axis) for axis in ("dp", "ctx", "tp")}
    count = sum(n - 1 for n in sizes.values())
    vmem = pl.BlockSpec(memory_space=pltpu.VMEM)
    return pl.pallas_call(
        functools.partial(gains_kernel, sizes),
        out_shape=jax.ShapeDtypeStruct(x.shape, F32),
        in_specs=[vmem],
        out_specs=vmem,
        scratch_shapes=[pltpu.VMEM((3,) + x.shape, F32)]
        + [pltpu.VMEM((max(n - 1, 1),) + x.shape, F32) for n in sizes.values()]
        + [pltpu.SemaphoreType.DMA((count,)), pltpu.SemaphoreType.DMA((count,))],
        name="sum_gains",
        compiler_params=pltpu.CompilerParams(collective_id=5, has_side_effects=True),
    )(x)


NT = (((1,), (1,)), ((), ()))
NN = (((1,), (0,)), ((), ()))
TN = (((0,), (0,)), ((), ()))


def dot(a, b, dims):
    return lax.dot_general(a, b, dims, preferred_element_type=F32)


def turn(x):
    return pltpu.roll(x, x.shape[-1] // 2, axis=1)


def prepared(x, gain, cosine, sine):
    normed, plain, inverse = rms_forward(x, gain)
    return (normed * cosine + turn(normed) * sine).astype(BF16), plain, inverse


def soft_weights(scale, bq, q, k):
    rows = pl.program_id(2) * bq + lax.broadcasted_iota(jnp.int32, (bq, k.shape[0]), 0)
    cols = lax.broadcasted_iota(jnp.int32, (bq, k.shape[0]), 1)
    scores = jnp.where(cols <= rows, dot(q, k, NT) * scale, -jnp.inf)
    weights = jnp.exp(scores - jnp.max(scores, axis=-1, keepdims=True))
    return weights, jnp.sum(weights, axis=-1, keepdims=True)


def attend_kernel(
    scale, bq, q_ref, k_ref, v_ref, cq_ref, sq_ref, ck_ref, sk_ref, qg_ref, kg_ref, o_ref, k_rot
):
    @pl.when((pl.program_id(1) == 0) & (pl.program_id(2) == 0))
    def _():
        k_rot[...] = prepared(k_ref[...], kg_ref[...], ck_ref[...], sk_ref[...])[0]

    q = prepared(q_ref[...], qg_ref[...], cq_ref[...], sq_ref[...])[0]
    weights, total = soft_weights(scale, bq, q, k_rot[...])
    o_ref[...] = (dot(weights.astype(BF16), v_ref[...], NN) / total).astype(BF16)


def attend_back_kernel(
    scale,
    bq,
    q_ref,
    k_ref,
    v_ref,
    cq_ref,
    sq_ref,
    ck_ref,
    sk_ref,
    qg_ref,
    kg_ref,
    o_ref,
    do_ref,
    dq_ref,
    dk_ref,
    dv_ref,
    qp_ref,
    kp_ref,
    k_rot,
    dk_sum,
    dv_sum,
):
    head, member, block = pl.program_id(0), pl.program_id(1), pl.program_id(2)

    @pl.when((head == 0) & (member == 0) & (block == 0))
    def _():
        qp_ref[...] = jnp.zeros_like(qp_ref)
        kp_ref[...] = jnp.zeros_like(kp_ref)

    @pl.when((member == 0) & (block == 0))
    def _():
        k_rot[...] = prepared(k_ref[...], kg_ref[...], ck_ref[...], sk_ref[...])[0]
        dk_sum[...] = jnp.zeros_like(dk_sum)
        dv_sum[...] = jnp.zeros_like(dv_sum)

    q, plain, inverse = prepared(q_ref[...], qg_ref[...], cq_ref[...], sq_ref[...])
    k, do = k_rot[...], do_ref[...]
    weights, total = soft_weights(scale, bq, q, k)
    probs = weights / total
    delta = jnp.sum(do.astype(F32) * o_ref[...].astype(F32), axis=-1, keepdims=True)
    dscore = (probs * (dot(do, v_ref[...], NT) - delta)).astype(BF16)
    dk_sum[...] += dot(dscore, q, TN) * scale
    dv_sum[...] += dot(probs.astype(BF16), do, TN)
    grad = dot(dscore, k, NN) * scale
    grad = grad * cq_ref[...] - turn(grad) * sq_ref[...]
    qp_ref[...] += jnp.sum(grad * plain, axis=0, keepdims=True)
    dq_ref[...] = rms_backward(grad, plain, inverse, qg_ref[...]).astype(BF16)

    @pl.when((member == pl.num_programs(1) - 1) & (block == pl.num_programs(2) - 1))
    def _():
        _, k_plain, k_inverse = prepared(k_ref[...], kg_ref[...], ck_ref[...], sk_ref[...])
        grad_k = dk_sum[...]
        grad_k = grad_k * ck_ref[...] - turn(grad_k) * sk_ref[...]
        kp_ref[...] += jnp.sum(grad_k * k_plain, axis=0, keepdims=True)
        dk_ref[...] = rms_backward(grad_k, k_plain, k_inverse, kg_ref[...]).astype(BF16)
        dv_ref[...] = dv_sum[...].astype(BF16)


def attention(scale, group, query, keys, values, cosine, sine, query_gain, key_gain, *back):
    length, kv_width = keys.shape
    head_dim = cosine.shape[-1]
    kv_heads = kv_width // head_dim
    bq = min(length, 256)
    rows = pl.BlockSpec((bq, head_dim), lambda h, g, i: (i, h * group + g))
    keyed = pl.BlockSpec((length, head_dim), lambda h, g, i: (0, h))
    table_q = pl.BlockSpec((bq, head_dim), lambda h, g, i: (i, 0))
    table_k = pl.BlockSpec((length, head_dim), lambda h, g, i: (0, 0))
    flat = pl.BlockSpec((1, head_dim), lambda h, g, i: (0, 0))
    wide = jax.ShapeDtypeStruct((length, kv_width * group), BF16)
    narrow = jax.ShapeDtypeStruct((length, kv_width), BF16)
    part = jax.ShapeDtypeStruct((1, head_dim), F32)
    work = 2 * length * length * head_dim * kv_heads * group
    scratch = [pltpu.VMEM((length, head_dim), BF16)]
    if back:
        scratch += [pltpu.VMEM((length, head_dim), F32)] * 2
    return pl.pallas_call(
        functools.partial(attend_back_kernel if back else attend_kernel, scale, bq),
        grid=(kv_heads, group, length // bq),
        out_shape=(wide, narrow, narrow, part, part) if back else wide,
        in_specs=[rows, keyed, keyed, table_q, table_q, table_k, table_k, flat, flat]
        + [rows] * len(back),
        out_specs=(rows, keyed, keyed, flat, flat) if back else rows,
        scratch_shapes=scratch,
        name="attend_back" if back else "attend",
        cost_estimate=pl.CostEstimate(
            flops=work * (5 if back else 2), bytes_accessed=4 * length * 1024, transcendentals=0
        ),
        compiler_params=pltpu.CompilerParams(vmem_limit_bytes=40 * 2**20),
    )(
        query,
        keys,
        values,
        cosine,
        sine,
        cosine,
        sine,
        query_gain.reshape(1, -1),
        key_gain.reshape(1, -1),
        *back,
    )


def on_device(
    block_input,
    input_gain,
    query_weight,
    key_weight,
    value_weight,
    query_gain,
    key_gain,
    out_weight,
    post_gain,
    gate_weight,
    up_weight,
    down_weight,
    grad_output,
):
    local_rows, seq_local, width = block_input.shape
    assert seq_local == 1 and lax.axis_size("dp") == 2
    layers = input_gain.shape[0]
    head_dim = query_gain.shape[-1]
    heads = query_weight.shape[-1] // head_dim
    kv_heads = key_weight.shape[-1] // head_dim
    n_ctx, n_tp = lax.axis_size("ctx"), lax.axis_size("tp")
    block_rows = local_rows * n_tp
    length = block_rows * n_ctx
    scale = head_dim ** (-0.5)
    first_row = lax.axis_index("ctx") * block_rows
    cosine, sine = rope_tables(jnp.arange(length, dtype=F32), head_dim)
    piece = width // (2 * n_ctx)
    my_cols = (lax.axis_index("dp") * n_ctx + lax.axis_index("ctx")) * piece
    other_cols = ((1 - lax.axis_index("dp")) * n_ctx + lax.axis_index("ctx")) * piece
    swap = [(0, 1), (1, 0)]

    def mine(x):
        return lax.dynamic_slice_in_dim(x, first_row, block_rows, 0)

    def slices(x):
        parts = [lax.dynamic_slice_in_dim(x, at, piece, 1) for at in (my_cols, other_cols)]
        return jnp.concatenate(parts, axis=1)

    def settle(grad, axis):
        own, other = jnp.split(grad, 2, axis=axis)
        return own + lax.ppermute(other.astype(BF16), "dp", swap).astype(F32)

    def settle_rows(*products):
        other = [x[piece:].astype(BF16) for x in products]
        other = lax.ppermute(jnp.concatenate(other, axis=1), "dp", swap).astype(F32)
        out = []
        at = 0
        for x in products:
            out.append(x[:piece] + other[:, at : at + x.shape[1]])
            at += x.shape[1]
        return out

    hidden = block_input[:, 0]
    grad_hidden = grad_output[:, 0]
    grad_rows = lax.all_gather(grad_hidden.astype(BF16), ("ctx", "tp"), axis=0, tiled=True)
    (first_in,) = boundary("first", hidden, input_gain[0])
    kept = []
    for l in range(layers):
        query = dot(first_in, query_weight[l], NN)
        keys = dot(first_in, key_weight[l], NN)
        values = dot(first_in, value_weight[l], NN).astype(BF16)
        attend_args = (scale, heads // kv_heads, query, keys, values, cosine, sine)
        attend_args += (query_gain[l], key_gain[l])
        attended = attention(*attend_args)
        partial = dot(mine(attended), out_weight[l], NN).astype(BF16)
        mixed, second_in = boundary("fwd", hidden, post_gain[l], partial)
        gate = dot(second_in, gate_weight[l], NN)
        upward = dot(second_in, up_weight[l], NN)
        swish = (jax.nn.silu(gate) * upward).astype(BF16)
        partial = dot(mine(swish), down_weight[l], NN).astype(BF16)
        kept.append(
            (hidden, first_in, attend_args, attended, mixed, second_in, gate, upward, swish)
        )
        if l + 1 < layers:
            hidden, first_in = boundary("fwd", mixed, input_gain[l + 1], partial)
        else:
            hidden = mixed + lax.psum_scatter(
                partial, "tp", scatter_dimension=0, tiled=True
            ).astype(F32)

    grads = [None] * layers
    gains = [None] * layers
    for l in reversed(range(layers)):
        x_in, first_in, attend_args, attended, mixed, second_in, gate, upward, swish = kept[l]
        grad_swish = dot(grad_rows, down_weight[l], NT)
        sigma = jax.nn.sigmoid(gate)
        grad_gate = (grad_swish * upward * (sigma * (1.0 + gate * (1.0 - sigma)))).astype(BF16)
        grad_up = (grad_swish * (gate * sigma)).astype(BF16)
        partial = dot(mine(grad_gate), gate_weight[l], NT) + dot(mine(grad_up), up_weight[l], NT)
        grad_mixed, post_part, mixed_rows = boundary(
            "bwd", mixed, post_gain[l], partial.astype(BF16), grad_hidden
        )
        second_cols = slices(second_in)
        down_grad = settle(dot(swish, slices(grad_rows), TN), 1)
        gate_grad, up_grad = settle_rows(
            dot(second_cols, grad_gate, TN), dot(second_cols, grad_up, TN)
        )

        grad_heads = dot(mixed_rows, out_weight[l], NT).astype(BF16)
        out_grad = settle(dot(attended, slices(mixed_rows), TN), 1)
        query_bf, key_bf, value_bf, q_part, k_part = attention(*attend_args, attended, grad_heads)
        partial = (
            dot(mine(query_bf), query_weight[l], NT)
            + dot(mine(key_bf), key_weight[l], NT)
            + dot(mine(value_bf), value_weight[l], NT)
        ).astype(BF16)
        if l:
            grad_hidden, input_part, grad_rows = boundary(
                "bwd", x_in, input_gain[l], partial, grad_mixed
            )
        else:
            grad_hidden, input_part = boundary(
                "bwd_last", x_in, input_gain[l], partial, grad_mixed
            )
        first_cols = slices(first_in)
        query_grad, key_grad, value_grad = settle_rows(
            dot(first_cols, query_bf, TN),
            dot(first_cols, key_bf, TN),
            dot(first_cols, value_bf, TN),
        )
        grads[l] = (query_grad, key_grad, value_grad, out_grad, gate_grad, up_grad, down_grad)
        gains[l] = (input_part[0], q_part[0] / n_ctx, k_part[0] / n_ctx, post_part[0])
    stacked = [jnp.stack([part[m] for part in grads]) for m in range(7)]
    packed = jnp.concatenate([v for part in gains for v in part])
    sizes = [v.shape[0] for part in gains for v in part]
    padded = -(-packed.shape[0] // 1024) * 1024
    packed = jnp.pad(packed, (0, padded - packed.shape[0])).reshape(-1, 128)
    summed = sum_gains(packed).reshape(-1)
    pieces = []
    at = 0
    for size in sizes:
        pieces.append(summed[at : at + size])
        at += size
    gains = [jnp.stack([pieces[4 * l + m] for l in range(layers)]) for m in range(4)]
    return (
        hidden[:, None],
        grad_hidden[:, None],
        gains[0],
        stacked[0],
        stacked[1],
        stacked[2],
        gains[1],
        gains[2],
        stacked[3],
        gains[3],
        stacked[4],
        stacked[5],
        stacked[6],
    )


def solution(mesh):
    placed = (
        P(("ctx", "tp"), "dp", None),
        P(),
        P(None, None, "tp"),
        P(None, None, "tp"),
        P(None, None, "tp"),
        P(),
        P(),
        P(None, "tp", None),
        P(),
        P(None, None, "tp"),
        P(None, None, "tp"),
        P(None, "tp", None),
        P(("ctx", "tp"), "dp", None),
    )
    return jax.shard_map(
        on_device,
        mesh=mesh,
        in_specs=placed,
        out_specs=(
            P(("ctx", "tp"), "dp", None),
            P(("ctx", "tp"), "dp", None),
            P(),
            P(None, ("dp", "ctx"), "tp"),
            P(None, ("dp", "ctx"), "tp"),
            P(None, ("dp", "ctx"), "tp"),
            P(),
            P(),
            P(None, "tp", ("dp", "ctx")),
            P(),
            P(None, ("dp", "ctx"), "tp"),
            P(None, ("dp", "ctx"), "tp"),
            P(None, "tp", ("dp", "ctx")),
        ),
        check_vma=False,
    )
```
